32 devices in a mesh: clips: 2 (over y), row: 4 (over x, core), col: 4 (over z).
Axes of the slice: x: 2, y: 2, z: 4, core: 2. Of those that a mesh axis runs over, the one named last changes fastest.
Arguments:
- clip_tokens: bfloat16 [2048, 6144], P(('clips', 'col'), 'row'), parts along dimension 0, may hold values from -12 to 12
- modulation: float32 [8, 6, 6144], P('clips', None, 'row'), parts along dimension 0, may hold values from -3 to 3
- w_qkv: bfloat16 [6144, 3, 4096], P('row', None, 'col'), may hold values from -3 to 3
- w_out: bfloat16 [4096, 6144], P('col', 'row'), may hold values from -0.09375 to 0.09375
- w_up: bfloat16 [6144, 12288], P('row', 'col'), may hold values from -0.078125 to 0.078125
- up_bias: float32 [12288], P('col'), may hold values from -3 to 3
- w_down: bfloat16 [12288, 6144], P('col', 'row'), may hold values from -0.0546875 to 0.0546875
- guide_num: int32 [8], P('clips'), parts along dimension 0, may hold values from -3 to 10, as said below
Outputs:
- guided: bfloat16 [512, 6144], P(('clips', 'col'), 'row'), parts along dimension 0
The draws below stay inside these ranges and needn't reach their ends.
There are 2 independent parts, one for each index of `clips`. The reference program is written for one: setup_inputs(seed, part) draws one part's arguments, and reference() takes and returns one part's arrays. A program takes and returns all parts, laid end to end along the dimension named above; an argument that names none is the same for every part. Nothing has to cross between parts.
Inputs may be any that keep to these rules, and one draw needn't show every extreme that they name: `guide_num`: the three negative numerators are -1, -2 and -3 in some order, and the positive one makes the four sum to 4.
All inputs are finite; a program needn't handle non-finite values.
Results may differ from the reference program's by a relative error of at most 0.019.
Values may be sent and summed in bfloat16 or wider, within the bound.
A program may use at most 128 MiB of HBM per device.

```python
import math
import jax
import jax.numpy as jnp
from jax import lax

D = 6144
HEADS = 32
HEAD_DIM = 128
FF = 12288
BRANCHES = 4
SEQ = 256
TOKENS = 1024
INNER = 4096
N_ROW = 4
N_COL = 4


def draw_guide_num(key, part):
    shuffled = jax.random.permutation(key, BRANCHES - 1).astype(jnp.int32) + 1
    positive = 4 + jnp.sum(shuffled)
    return jnp.concatenate([positive[None], -shuffled]).astype(jnp.int32)


def draw_clip_tokens(key, part):
    array_shape = (TOKENS, D)
    position = jnp.arange(D, dtype=jnp.float32) / float(max(D - 1, 1))
    entries = jax.random.truncated_normal(jax.random.fold_in(key, 21), -6.0, 6.0, array_shape, jnp.float32)
    row_scale = jnp.ones((TOKENS, 1), jnp.float32)
    low_end = 0.25
    high_end = 1.5
    rough = jnp.exp(jax.random.uniform(jax.random.fold_in(key, 25), (D,), jnp.float32, math.log(0.75), 0.0))
    column_scale = low_end * jnp.exp(position * math.log(high_end / low_end)) * rough
    copied = jax.random.randint(jax.random.fold_in(key, 23), (TOKENS, 1), 0, 32) == 0
    jitter = 0.15 * jax.random.truncated_normal(jax.random.fold_in(key, 24), -4.0, 4.0, array_shape, jnp.float32)
    earlier = jnp.roll(entries, BRANCHES, axis=0)
    earlier_scale = jnp.roll(row_scale, BRANCHES, axis=0)
    entries = jnp.where(copied, earlier + jitter, entries)
    row_scale = jnp.where(copied, earlier_scale, row_scale)
    return (entries * row_scale * column_scale[None]).astype(jnp.bfloat16)


def draw_w_qkv(key, part):
    array_shape = (D, 3, INNER)
    entries = jax.random.truncated_normal(jax.random.fold_in(key, 11), -4.0, 4.0, array_shape, jnp.float32)
    entries = entries / jnp.sqrt(jnp.float32(D))
    shuffled = jax.random.permutation(jax.random.fold_in(key, 12), HEADS).astype(jnp.int32)
    head_rank = jnp.argsort(shuffled).astype(jnp.int32)
    hot_count = max(HEADS // 8, 1)
    hot_heads = head_rank < hot_count
    spread = head_rank.astype(jnp.float32) / float(max(hot_count - 1, 1))
    factor = jnp.where(hot_heads, 2.6 + 1.6 * spread, 1.0)
    column_factor = jnp.repeat(factor, HEAD_DIM)
    hot_columns = jnp.repeat(hot_heads, HEAD_DIM)
    query_part = entries[:, 0] * column_factor[None]
    key_part = jnp.where(hot_columns[None], query_part, entries[:, 1])
    return jnp.stack([query_part, key_part, entries[:, 2]], axis=1).astype(jnp.bfloat16)


def steps_of(own_key, shape, split, smallest, top_value):
    loudness, own = 1.0, jax.random.fold_in(own_key, 6)
    for dim, parts in split:
        heights = jnp.exp(jax.random.uniform(jax.random.fold_in(own, dim), (parts,), jnp.float32, smallest / len(split), top_value / len(split)))
        loudness = loudness * jnp.repeat(heights, shape[dim] // parts).reshape([-1 if axis == dim else 1 for axis in range(len(shape))])
    return loudness


def centred(own_key, extent, scale, reach, pieces=(), held_as=jnp.bfloat16):
    array = scale * jax.random.normal(own_key, extent, jnp.float32)
    if pieces:
        array = array * steps_of(own_key, extent, pieces, -0.22, 0.18)
    return jnp.clip(array, -reach, reach).astype(held_as)


def setup_inputs(seed: int = 0, part: int = 0) -> dict:
    arg_keys = jax.random.split(jax.random.key(seed), 9)
    own_keys = jax.random.split(jax.random.fold_in(arg_keys[8], part), 9)
    clip_tokens = draw_clip_tokens(jax.random.fold_in(jax.random.fold_in(arg_keys[8], part), 71), part)
    modulation = centred(own_keys[1], (BRANCHES, 6, D), 0.5, 3.0, ((2, 4),), jnp.float32)
    w_qkv = draw_w_qkv(jax.random.fold_in(arg_keys[8], 71), part)
    w_out = centred(arg_keys[3], (INNER, D), INNER ** -0.5, 0.09375, ((0, 4), (1, 4)))
    w_up = centred(arg_keys[4], (D, FF), D ** -0.5, 0.078125, ((0, 4), (1, 4)))
    up_bias = centred(arg_keys[5], (FF,), 0.5, 3.0, ((0, 4),), jnp.float32)
    w_down = centred(arg_keys[6], (FF, D), FF ** -0.5, 0.0546875, ((0, 4), (1, 4)))
    guide_num = draw_guide_num(jax.random.fold_in(jax.random.fold_in(arg_keys[8], part), 71), part)
    return dict(clip_tokens=clip_tokens, modulation=modulation, w_qkv=w_qkv, w_out=w_out, w_up=w_up, up_bias=up_bias, w_down=w_down, guide_num=guide_num)


eps = 1e-06

def normalize(values, shift, scale):
    total = lax.optimization_barrier(jnp.sum(values, axis=1))
    squares = lax.optimization_barrier(jnp.sum(values * values, axis=1))
    mean = total / D
    variance = squares / D - mean * mean
    normed = (values - mean[:, None]) * lax.rsqrt(variance + eps)[:, None]
    shaped = normed.reshape(-1, BRANCHES, values.shape[1]) * (1.0 + scale[None]) + shift[None]
    return shaped.reshape(values.shape)

def blocked(inputs, weight, blocks, mixer):
    rows, depth = inputs.shape
    span = depth // blocks
    stacked_in = inputs.reshape(rows, blocks, span).transpose(1, 0, 2)
    stacked_w = weight.reshape(blocks, span, weight.shape[1])
    start_total = mixer(jnp.zeros((rows, weight.shape[1]), jnp.float32))

    def step(total, pair):
        term = mixer(jnp.dot(pair[0], pair[1], preferred_element_type=jnp.float32))
        term = lax.optimization_barrier(term.astype(jnp.bfloat16)).astype(jnp.float32)
        return (total + term, None)
    result, unused = lax.scan(step, start_total, (stacked_in, stacked_w))
    return result

def keep_rows(values):
    return values

def attend(triple):
    query, keys, values = triple
    scores = jnp.einsum('qhd,khd->hqk', query.astype(jnp.float32), keys.astype(jnp.float32)) / jnp.sqrt(jnp.float32(HEAD_DIM))
    top = lax.optimization_barrier(jnp.max(scores, axis=-1, keepdims=True))
    weights = jnp.exp(scores - top)
    denom = lax.optimization_barrier(jnp.sum(weights, axis=-1))
    rounded = lax.optimization_barrier(weights.astype(jnp.bfloat16)).astype(jnp.float32)
    mixed = jnp.einsum('hqk,khd->qhd', rounded, values.astype(jnp.float32))
    return mixed / jnp.transpose(denom)[:, :, None]

def reference(clip_tokens, modulation, w_qkv, w_out, w_up, up_bias, w_down, guide_num):
    x_rows = clip_tokens.astype(jnp.float32)
    first = normalize(x_rows, modulation[:, 0], modulation[:, 1]).astype(jnp.bfloat16)
    qkv = blocked(first, w_qkv.reshape(D, 3 * INNER), N_ROW, keep_rows).astype(jnp.bfloat16)

    def split_heads(block):
        return block.reshape(SEQ, BRANCHES, HEADS, HEAD_DIM).transpose(1, 0, 2, 3)
    query = split_heads(qkv[:, :INNER])
    keys = split_heads(qkv[:, INNER:2 * INNER])
    values = split_heads(qkv[:, 2 * INNER:])
    mixed = lax.map(attend, (query, keys, values))
    att = mixed.transpose(1, 0, 2, 3).reshape(TOKENS, INNER).astype(jnp.bfloat16)
    out_rows = blocked(att, w_out, N_COL, keep_rows)
    gate_one = jnp.tile(modulation[:, 2], (SEQ, 1))
    resid = x_rows + gate_one * out_rows
    second = normalize(resid, modulation[:, 3], modulation[:, 4]).astype(jnp.bfloat16)
    up_rows = blocked(second, w_up, N_ROW, keep_rows)
    act = jax.nn.gelu(up_rows + up_bias[None], approximate=True).astype(jnp.bfloat16)
    guide_weights = guide_num.astype(jnp.float32) / 4.0
    weights_gate = guide_weights[:, None] * modulation[:, 5]

    def combine(partial_rows):
        return lax.optimization_barrier(jnp.sum(partial_rows.reshape(SEQ, BRANCHES, D) * weights_gate[None], axis=1))
    mlp_rows = blocked(act, w_down, N_COL, combine)
    resid_mix = lax.optimization_barrier(jnp.sum(resid.reshape(SEQ, BRANCHES, D) * guide_weights[None, :, None], axis=1))
    return (resid_mix + mlp_rows).astype(jnp.bfloat16)
```

```python
import jax
import jax.numpy as jnp
from jax import lax
from jax.sharding import PartitionSpec as P

D = 6144
HEAD_DIM = 128


eps = 1e-06


def normalize(values, shift, scale):
    totals = lax.psum((jnp.sum(values, axis=1), jnp.sum(values * values, axis=1)), "row")
    mean = totals[0] / D
    variance = totals[1] / D - mean * mean
    normed = (values - mean[:, None]) * lax.rsqrt(variance + eps)[:, None]
    branches = shift.shape[0]
    shaped = normed.reshape(-1, branches, values.shape[1]) * (1.0 + scale[None]) + shift[None]
    return shaped.reshape(values.shape)


def general_layer(clip_tokens, modulation, w_qkv, w_out, w_up, up_bias, w_down, guide_num):
    branches = modulation.shape[0]
    feat_rows = w_qkv.shape[0]
    head_cols = w_qkv.shape[2]
    heads_here = head_cols // HEAD_DIM
    x_rows = clip_tokens.astype(jnp.float32)
    first = normalize(x_rows, modulation[:, 0], modulation[:, 1]).astype(jnp.bfloat16)
    w_flat = w_qkv.reshape(feat_rows, 3 * head_cols)
    partial_qkv = jnp.dot(
        lax.all_gather(first, "col", axis=0, tiled=True), w_flat, preferred_element_type=jnp.float32
    )
    scale_score = 1.0 / jnp.sqrt(jnp.float32(HEAD_DIM))
    qkv = lax.psum_scatter(partial_qkv.astype(jnp.bfloat16), "row", scatter_dimension=0, tiled=True)
    query3 = qkv[:, :head_cols].reshape(-1, heads_here, HEAD_DIM)
    query_rows = query3.shape[0]
    piece = (
        lax.all_gather(qkv[:, head_cols : 2 * head_cols], "row", axis=0, tiled=True),
        lax.all_gather(qkv[:, 2 * head_cols :], "row", axis=0, tiled=True),
    )
    top = jnp.full((heads_here, query_rows), -1e30, jnp.float32)
    rows = piece[0].shape[0]
    key_heads = piece[0].reshape(rows, heads_here, HEAD_DIM)
    value_heads = piece[1].reshape(rows, heads_here, HEAD_DIM)
    scores = (
        jnp.einsum("qhd,khd->hqk", query3, key_heads, preferred_element_type=jnp.float32)
        * scale_score
    )
    query_branch = jnp.arange(query3.shape[0], dtype=jnp.int32) % branches
    key_branch = jnp.arange(rows, dtype=jnp.int32) % branches
    allowed = (query_branch[:, None] == key_branch[None, :])[None]
    masked = jnp.where(allowed, scores, -1e30)
    new_top = jnp.maximum(top, jnp.max(masked, axis=-1))
    weights = jnp.where(allowed, jnp.exp(masked - new_top[..., None]), 0.0)
    denom = jnp.sum(weights, axis=-1)
    accum = jnp.einsum(
        "hqk,khd->hqd",
        weights.astype(jnp.bfloat16),
        value_heads,
        preferred_element_type=jnp.float32,
    )
    att = (accum / denom[..., None]).transpose(1, 0, 2).reshape(-1, head_cols).astype(jnp.bfloat16)
    partial_out = jnp.dot(
        lax.all_gather(att, "row", axis=0, tiled=True), w_out, preferred_element_type=jnp.float32
    )
    out_rows = lax.psum_scatter(
        partial_out.astype(jnp.bfloat16), "col", scatter_dimension=0, tiled=True
    ).astype(jnp.float32)
    by_branch = x_rows.shape[0] // branches
    resid = (
        x_rows.reshape(by_branch, branches, feat_rows)
        + modulation[None, :, 2] * out_rows.reshape(by_branch, branches, feat_rows)
    ).reshape(x_rows.shape)
    second = normalize(resid, modulation[:, 3], modulation[:, 4]).astype(jnp.bfloat16)
    partial_up = jnp.dot(
        lax.all_gather(second, "col", axis=0, tiled=True), w_up, preferred_element_type=jnp.float32
    )
    up_rows = lax.psum_scatter(
        partial_up.astype(jnp.bfloat16), "row", scatter_dimension=0, tiled=True
    ).astype(jnp.float32)
    act = jax.nn.gelu(up_rows + up_bias[None], approximate=True).astype(jnp.bfloat16)
    partial_down = jnp.dot(
        lax.all_gather(act, "row", axis=0, tiled=True), w_down, preferred_element_type=jnp.float32
    )
    guide_weights = guide_num.astype(jnp.float32) / 4.0
    weights_gate = guide_weights[:, None] * modulation[:, 5]
    combined = jnp.sum(partial_down.reshape(-1, branches, feat_rows) * weights_gate[None], axis=1)
    mlp_rows = lax.psum_scatter(
        combined.astype(jnp.bfloat16), "col", scatter_dimension=0, tiled=True
    ).astype(jnp.float32)
    resid_mix = jnp.sum(
        resid.reshape(by_branch, branches, feat_rows) * guide_weights[None, :, None], axis=1
    )
    return (resid_mix + mlp_rows).astype(jnp.bfloat16)


BF = jnp.bfloat16


def swap_row(value, distance):
    size = lax.axis_size("row")
    return lax.ppermute(value, "row", [(r, r ^ distance) for r in range(size)])


def sum_over_row(value):
    value = value + swap_row(value, 1)
    return value + swap_row(value, 2)


def scatter_row(pieces):
    me = lax.axis_index("row")
    half, core = me // 2, me % 2
    mine = lax.dynamic_index_in_dim(pieces, core, 1, keepdims=False)
    theirs = lax.dynamic_index_in_dim(pieces, 1 - core, 1, keepdims=False)
    got = swap_row(theirs, 1)
    away = lax.dynamic_index_in_dim(mine, 1 - half, 0, keepdims=False).astype(
        jnp.float32
    ) + lax.dynamic_index_in_dim(got, 1 - half, 0, keepdims=False).astype(jnp.float32)
    came = swap_row(away.astype(BF), 2)
    kept = lax.dynamic_index_in_dim(mine, half, 0, keepdims=False).astype(
        jnp.float32
    ) + lax.dynamic_index_in_dim(got, half, 0, keepdims=False).astype(jnp.float32)
    return kept + came.astype(jnp.float32)


def gather_row(value):
    me = lax.axis_index("row")
    half, core = me // 2, me % 2
    other = swap_row(value, 2)
    pair = jnp.where(half == 0, jnp.stack([value, other]), jnp.stack([other, value]))
    beside = swap_row(pair, 1)
    return jnp.where(
        core == 0, jnp.stack([pair, beside], axis=1), jnp.stack([beside, pair], axis=1)
    )


def moments(values):
    return jnp.stack([jnp.sum(values, axis=1), jnp.sum(values * values, axis=1)])


def apply_norm(values, totals, shift, scale):
    mean = totals[0] / D
    variance = totals[1] / D - mean * mean
    normed = (values - mean[:, None]) * lax.rsqrt(variance + eps)[:, None]
    return (normed * (1.0 + scale[None]) + shift[None]).astype(BF)


def attend(q, k, v):
    scores = jnp.einsum("qhd,khd->hqk", q, k, preferred_element_type=jnp.float32)
    scores = scores / jnp.sqrt(jnp.float32(HEAD_DIM))
    weights = jnp.exp(scores - jnp.max(scores, axis=-1, keepdims=True))
    denom = jnp.sum(weights, axis=-1)
    mixed = jnp.einsum(
        "hqk,khd->hqd", weights.astype(BF), v, preferred_element_type=jnp.float32
    )
    mixed = mixed / denom[..., None]
    return mixed.transpose(1, 0, 2).reshape(q.shape[0], -1).astype(BF)


def branch_layer(clip_tokens, modulation, w_qkv, w_out, w_up, up_bias, w_down, guide_num):
    branches = modulation.shape[0]
    feat_rows, _, head_cols = w_qkv.shape
    here = clip_tokens.shape[0] // branches
    w_flat = w_qkv.reshape(feat_rows, 3 * head_cols)
    by_branch = clip_tokens.reshape(here, branches, feat_rows).transpose(1, 0, 2)
    mine = head_cols // 4
    guide = guide_num.astype(jnp.float32) / 4.0
    total = None
    mixed = None
    for b in range(branches):
        x = by_branch[b]
        x_all = lax.all_gather(x, "col", axis=0, tiled=True).astype(jnp.float32)
        tokens = x_all.shape[0]
        first = apply_norm(x_all, sum_over_row(moments(x_all)), modulation[b, 0], modulation[b, 1])
        partial = jnp.dot(first, w_flat, preferred_element_type=jnp.float32).astype(BF)
        pieces = partial.reshape(tokens, 3, 2, 2, mine).transpose(2, 3, 1, 0, 4)
        qkv = scatter_row(pieces).astype(BF).reshape(3, tokens, mine // HEAD_DIM, HEAD_DIM)
        att = attend(qkv[0], qkv[1], qkv[2])
        att_all = gather_row(att).reshape(4, tokens, mine).transpose(1, 0, 2).reshape(tokens, -1)
        partial = jnp.dot(att_all, w_out, preferred_element_type=jnp.float32).astype(BF)
        out = lax.psum_scatter(partial, "col", scatter_dimension=0, tiled=True)
        resid = x.astype(jnp.float32) + modulation[b, 2][None] * out.astype(jnp.float32)
        second = apply_norm(resid, sum_over_row(moments(resid)), modulation[b, 3], modulation[b, 4])
        second_all = lax.all_gather(second, "col", axis=0, tiled=True)
        partial = jnp.dot(second_all, w_up, preferred_element_type=jnp.float32).astype(BF)
        up = scatter_row(partial.reshape(2, 2, tokens // 4, -1))
        act = jax.nn.gelu(up + up_bias[None], approximate=True).astype(BF)
        act_all = gather_row(act).reshape(tokens, -1)
        down = jnp.dot(act_all, w_down, preferred_element_type=jnp.float32)
        down = down * (guide[b] * modulation[b, 5])[None]
        total = down if total is None else total + down
        part = guide[b] * resid
        mixed = part if mixed is None else mixed + part
    mlp = lax.psum_scatter(total.astype(BF), "col", scatter_dimension=0, tiled=True)
    return (mixed + mlp.astype(jnp.float32)).astype(BF)


def on_device(*args):
    heads_here = args[2].shape[2] // HEAD_DIM
    if lax.axis_size("row") == 4 and heads_here % 4 == 0:
        return branch_layer(*args)
    return general_layer(*args)


def solution(mesh):
    in_specs = (
        P(("clips", "col"), "row"),
        P("clips", None, "row"),
        P("row", None, "col"),
        P("col", "row"),
        P("row", "col"),
        P("col"),
        P("col", "row"),
        P("clips"),
    )
    out_specs = P(("clips", "col"), "row")
    return jax.shard_map(
        on_device, mesh=mesh, in_specs=in_specs, out_specs=out_specs, check_vma=False
    )
```

```python
import jax
import jax.numpy as jnp
from jax import lax
from jax.sharding import PartitionSpec as P

D = 6144
HEAD_DIM = 128


eps = 1e-06


def normalize(values, shift, scale):
    totals = lax.psum((jnp.sum(values, axis=1), jnp.sum(values * values, axis=1)), "row")
    mean = totals[0] / D
    variance = totals[1] / D - mean * mean
    normed = (values - mean[:, None]) * lax.rsqrt(variance + eps)[:, None]
    branches = shift.shape[0]
    shaped = normed.reshape(-1, branches, values.shape[1]) * (1.0 + scale[None]) + shift[None]
    return shaped.reshape(values.shape)


def general_layer(clip_tokens, modulation, w_qkv, w_out, w_up, up_bias, w_down, guide_num):
    branches = modulation.shape[0]
    feat_rows = w_qkv.shape[0]
    head_cols = w_qkv.shape[2]
    heads_here = head_cols // HEAD_DIM
    x_rows = clip_tokens.astype(jnp.float32)
    first = normalize(x_rows, modulation[:, 0], modulation[:, 1]).astype(jnp.bfloat16)
    w_flat = w_qkv.reshape(feat_rows, 3 * head_cols)
    partial_qkv = jnp.dot(
        lax.all_gather(first, "col", axis=0, tiled=True), w_flat, preferred_element_type=jnp.float32
    )
    scale_score = 1.0 / jnp.sqrt(jnp.float32(HEAD_DIM))
    qkv = lax.psum_scatter(partial_qkv.astype(jnp.bfloat16), "row", scatter_dimension=0, tiled=True)
    query3 = qkv[:, :head_cols].reshape(-1, heads_here, HEAD_DIM)
    query_rows = query3.shape[0]
    piece = (
        lax.all_gather(qkv[:, head_cols : 2 * head_cols], "row", axis=0, tiled=True),
        lax.all_gather(qkv[:, 2 * head_cols :], "row", axis=0, tiled=True),
    )
    top = jnp.full((heads_here, query_rows), -1e30, jnp.float32)
    rows = piece[0].shape[0]
    key_heads = piece[0].reshape(rows, heads_here, HEAD_DIM)
    value_heads = piece[1].reshape(rows, heads_here, HEAD_DIM)
    scores = (
        jnp.einsum("qhd,khd->hqk", query3, key_heads, preferred_element_type=jnp.float32)
        * scale_score
    )
    query_branch = jnp.arange(query3.shape[0], dtype=jnp.int32) % branches
    key_branch = jnp.arange(rows, dtype=jnp.int32) % branches
    allowed = (query_branch[:, None] == key_branch[None, :])[None]
    masked = jnp.where(allowed, scores, -1e30)
    new_top = jnp.maximum(top, jnp.max(masked, axis=-1))
    weights = jnp.where(allowed, jnp.exp(masked - new_top[..., None]), 0.0)
    denom = jnp.sum(weights, axis=-1)
    accum = jnp.einsum(
        "hqk,khd->hqd",
        weights.astype(jnp.bfloat16),
        value_heads,
        preferred_element_type=jnp.float32,
    )
    att = (accum / denom[..., None]).transpose(1, 0, 2).reshape(-1, head_cols).astype(jnp.bfloat16)
    partial_out = jnp.dot(
        lax.all_gather(att, "row", axis=0, tiled=True), w_out, preferred_element_type=jnp.float32
    )
    out_rows = lax.psum_scatter(
        partial_out.astype(jnp.bfloat16), "col", scatter_dimension=0, tiled=True
    ).astype(jnp.float32)
    by_branch = x_rows.shape[0] // branches
    resid = (
        x_rows.reshape(by_branch, branches, feat_rows)
        + modulation[None, :, 2] * out_rows.reshape(by_branch, branches, feat_rows)
    ).reshape(x_rows.shape)
    second = normalize(resid, modulation[:, 3], modulation[:, 4]).astype(jnp.bfloat16)
    partial_up = jnp.dot(
        lax.all_gather(second, "col", axis=0, tiled=True), w_up, preferred_element_type=jnp.float32
    )
    up_rows = lax.psum_scatter(
        partial_up.astype(jnp.bfloat16), "row", scatter_dimension=0, tiled=True
    ).astype(jnp.float32)
    act = jax.nn.gelu(up_rows + up_bias[None], approximate=True).astype(jnp.bfloat16)
    partial_down = jnp.dot(
        lax.all_gather(act, "row", axis=0, tiled=True), w_down, preferred_element_type=jnp.float32
    )
    guide_weights = guide_num.astype(jnp.float32) / 4.0
    weights_gate = guide_weights[:, None] * modulation[:, 5]
    combined = jnp.sum(partial_down.reshape(-1, branches, feat_rows) * weights_gate[None], axis=1)
    mlp_rows = lax.psum_scatter(
        combined.astype(jnp.bfloat16), "col", scatter_dimension=0, tiled=True
    ).astype(jnp.float32)
    resid_mix = jnp.sum(
        resid.reshape(by_branch, branches, feat_rows) * guide_weights[None, :, None], axis=1
    )
    return (resid_mix + mlp_rows).astype(jnp.bfloat16)


BF = jnp.bfloat16


def swap_row(value, distance):
    size = lax.axis_size("row")
    return lax.ppermute(value, "row", [(r, r ^ distance) for r in range(size)])


def sum_over_row(value):
    value = value + swap_row(value, 1)
    return value + swap_row(value, 2)


def scatter_row(partial, axis):
    me = lax.axis_index("row")
    half, core = me // 2, me % 2
    span = partial.shape[axis] // 4

    def piece(index):
        return lax.dynamic_slice_in_dim(partial, index * span, span, axis)

    far = swap_row(piece((1 - half) * 2 + 1 - core), 1)
    near = swap_row(piece(half * 2 + 1 - core), 1)
    away = piece((1 - half) * 2 + core).astype(jnp.float32) + far.astype(jnp.float32)
    came = swap_row(away.astype(BF), 2)
    kept = piece(half * 2 + core).astype(jnp.float32) + near.astype(jnp.float32)
    return kept + came.astype(jnp.float32)


def gather_row(value, axis):
    me = lax.axis_index("row")
    half, core = me // 2, me % 2
    beside = swap_row(value, 1)
    other = swap_row(value, 2)
    across = swap_row(other, 1)

    def pick(x, c):
        same = jnp.where(core == c, value, beside)
        away = jnp.where(core == c, other, across)
        return jnp.where(half == x, same, away)

    return jnp.concatenate([pick(0, 0), pick(0, 1), pick(1, 0), pick(1, 1)], axis=axis)


def moments(values):
    return jnp.stack([jnp.sum(values, axis=1), jnp.sum(values * values, axis=1)])


def apply_norm(values, totals, shift, scale):
    mean = totals[0] / D
    variance = totals[1] / D - mean * mean
    normed = (values - mean[:, None]) * lax.rsqrt(variance + eps)[:, None]
    branches = shift.shape[0]
    shaped = normed.reshape(-1, branches, values.shape[1]) * (1.0 + scale[None]) + shift[None]
    return shaped.reshape(values.shape).astype(BF)


def attend(q, k, v):
    scores = jnp.einsum("qbhd,kbhd->bhqk", q, k, preferred_element_type=jnp.float32)
    scores = scores / jnp.sqrt(jnp.float32(HEAD_DIM))
    weights = jnp.exp(scores - jnp.max(scores, axis=-1, keepdims=True))
    denom = jnp.sum(weights, axis=-1)
    mixed = jnp.einsum(
        "bhqk,kbhd->bhqd", weights.astype(BF), v, preferred_element_type=jnp.float32
    )
    mixed = mixed / denom[..., None]
    return mixed.astype(BF).transpose(2, 0, 1, 3)


def head_layer(clip_tokens, modulation, w_qkv, w_out, w_up, up_bias, w_down, guide_num):
    branches = modulation.shape[0]
    feat_rows, _, head_cols = w_qkv.shape
    mine = head_cols // 4
    w_flat = w_qkv.reshape(feat_rows, 3, 4, mine).transpose(0, 2, 1, 3).reshape(feat_rows, -1)
    x_all = lax.all_gather(clip_tokens, "col", axis=0, tiled=True).astype(jnp.float32)
    tokens = x_all.shape[0]
    first = apply_norm(x_all, sum_over_row(moments(x_all)), modulation[:, 0], modulation[:, 1])
    partial = jnp.dot(first, w_flat, preferred_element_type=jnp.float32).astype(BF)
    qkv = scatter_row(partial, 1).astype(BF)
    q, k, v = (
        qkv[:, i * mine : (i + 1) * mine].reshape(-1, branches, mine // HEAD_DIM, HEAD_DIM)
        for i in range(3)
    )
    att_all = gather_row(attend(q, k, v).reshape(tokens, mine), 1)
    partial = jnp.dot(att_all, w_out, preferred_element_type=jnp.float32).astype(BF)
    out = lax.psum_scatter(partial, "col", scatter_dimension=0, tiled=True)
    x = clip_tokens.astype(jnp.float32)
    by_branch = x.shape[0] // branches
    resid = x.reshape(by_branch, branches, feat_rows) + modulation[None, :, 2] * out.astype(
        jnp.float32
    ).reshape(by_branch, branches, feat_rows)
    rows = resid.reshape(x.shape)
    second = apply_norm(rows, sum_over_row(moments(rows)), modulation[:, 3], modulation[:, 4])
    second_all = lax.all_gather(second, "col", axis=0, tiled=True)
    partial = jnp.dot(second_all, w_up, preferred_element_type=jnp.float32).astype(BF)
    up = scatter_row(partial, 0)
    act = jax.nn.gelu(up + up_bias[None], approximate=True).astype(BF)
    down = jnp.dot(gather_row(act, 0), w_down, preferred_element_type=jnp.float32)
    guide = guide_num.astype(jnp.float32) / 4.0
    gate = guide[:, None] * modulation[:, 5]
    total = jnp.sum(down.reshape(-1, branches, feat_rows) * gate[None], axis=1)
    mlp = lax.psum_scatter(total.astype(BF), "col", scatter_dimension=0, tiled=True)
    mixed = jnp.sum(resid * guide[None, :, None], axis=1)
    return (mixed + mlp.astype(jnp.float32)).astype(BF)


def on_device(*args):
    heads_here = args[2].shape[2] // HEAD_DIM
    if lax.axis_size("row") == 4 and heads_here % 4 == 0:
        return head_layer(*args)
    return general_layer(*args)


def solution(mesh):
    in_specs = (
        P(("clips", "col"), "row"),
        P("clips", None, "row"),
        P("row", None, "col"),
        P("col", "row"),
        P("row", "col"),
        P("col"),
        P("col", "row"),
        P("clips"),
    )
    out_specs = P(("clips", "col"), "row")
    return jax.shard_map(
        on_device, mesh=mesh, in_specs=in_specs, out_specs=out_specs, check_vma=False
    )
```

```python
import jax
import jax.numpy as jnp
from jax import lax
from jax.sharding import PartitionSpec as P

D = 6144
HEAD_DIM = 128


eps = 1e-06


def normalize(values, shift, scale):
    totals = lax.psum((jnp.sum(values, axis=1), jnp.sum(values * values, axis=1)), "row")
    mean = totals[0] / D
    variance = totals[1] / D - mean * mean
    normed = (values - mean[:, None]) * lax.rsqrt(variance + eps)[:, None]
    branches = shift.shape[0]
    shaped = normed.reshape(-1, branches, values.shape[1]) * (1.0 + scale[None]) + shift[None]
    return shaped.reshape(values.shape)


def general_layer(clip_tokens, modulation, w_qkv, w_out, w_up, up_bias, w_down, guide_num):
    branches = modulation.shape[0]
    feat_rows = w_qkv.shape[0]
    head_cols = w_qkv.shape[2]
    heads_here = head_cols // HEAD_DIM
    x_rows = clip_tokens.astype(jnp.float32)
    first = normalize(x_rows, modulation[:, 0], modulation[:, 1]).astype(jnp.bfloat16)
    w_flat = w_qkv.reshape(feat_rows, 3 * head_cols)
    partial_qkv = jnp.dot(
        lax.all_gather(first, "col", axis=0, tiled=True), w_flat, preferred_element_type=jnp.float32
    )
    scale_score = 1.0 / jnp.sqrt(jnp.float32(HEAD_DIM))
    qkv = lax.psum_scatter(partial_qkv.astype(jnp.bfloat16), "row", scatter_dimension=0, tiled=True)
    query3 = qkv[:, :head_cols].reshape(-1, heads_here, HEAD_DIM)
    query_rows = query3.shape[0]
    piece = (
        lax.all_gather(qkv[:, head_cols : 2 * head_cols], "row", axis=0, tiled=True),
        lax.all_gather(qkv[:, 2 * head_cols :], "row", axis=0, tiled=True),
    )
    top = jnp.full((heads_here, query_rows), -1e30, jnp.float32)
    rows = piece[0].shape[0]
    key_heads = piece[0].reshape(rows, heads_here, HEAD_DIM)
    value_heads = piece[1].reshape(rows, heads_here, HEAD_DIM)
    scores = (
        jnp.einsum("qhd,khd->hqk", query3, key_heads, preferred_element_type=jnp.float32)
        * scale_score
    )
    query_branch = jnp.arange(query3.shape[0], dtype=jnp.int32) % branches
    key_branch = jnp.arange(rows, dtype=jnp.int32) % branches
    allowed = (query_branch[:, None] == key_branch[None, :])[None]
    masked = jnp.where(allowed, scores, -1e30)
    new_top = jnp.maximum(top, jnp.max(masked, axis=-1))
    weights = jnp.where(allowed, jnp.exp(masked - new_top[..., None]), 0.0)
    denom = jnp.sum(weights, axis=-1)
    accum = jnp.einsum(
        "hqk,khd->hqd",
        weights.astype(jnp.bfloat16),
        value_heads,
        preferred_element_type=jnp.float32,
    )
    att = (accum / denom[..., None]).transpose(1, 0, 2).reshape(-1, head_cols).astype(jnp.bfloat16)
    partial_out = jnp.dot(
        lax.all_gather(att, "row", axis=0, tiled=True), w_out, preferred_element_type=jnp.float32
    )
    out_rows = lax.psum_scatter(
        partial_out.astype(jnp.bfloat16), "col", scatter_dimension=0, tiled=True
    ).astype(jnp.float32)
    by_branch = x_rows.shape[0] // branches
    resid = (
        x_rows.reshape(by_branch, branches, feat_rows)
        + modulation[None, :, 2] * out_rows.reshape(by_branch, branches, feat_rows)
    ).reshape(x_rows.shape)
    second = normalize(resid, modulation[:, 3], modulation[:, 4]).astype(jnp.bfloat16)
    partial_up = jnp.dot(
        lax.all_gather(second, "col", axis=0, tiled=True), w_up, preferred_element_type=jnp.float32
    )
    up_rows = lax.psum_scatter(
        partial_up.astype(jnp.bfloat16), "row", scatter_dimension=0, tiled=True
    ).astype(jnp.float32)
    act = jax.nn.gelu(up_rows + up_bias[None], approximate=True).astype(jnp.bfloat16)
    partial_down = jnp.dot(
        lax.all_gather(act, "row", axis=0, tiled=True), w_down, preferred_element_type=jnp.float32
    )
    guide_weights = guide_num.astype(jnp.float32) / 4.0
    weights_gate = guide_weights[:, None] * modulation[:, 5]
    combined = jnp.sum(partial_down.reshape(-1, branches, feat_rows) * weights_gate[None], axis=1)
    mlp_rows = lax.psum_scatter(
        combined.astype(jnp.bfloat16), "col", scatter_dimension=0, tiled=True
    ).astype(jnp.float32)
    resid_mix = jnp.sum(
        resid.reshape(by_branch, branches, feat_rows) * guide_weights[None, :, None], axis=1
    )
    return (resid_mix + mlp_rows).astype(jnp.bfloat16)


BF = jnp.bfloat16


def swap_row(value, distance):
    size = lax.axis_size("row")
    return lax.ppermute(value, "row", [(r, r ^ distance) for r in range(size)])


def sum_over_row(value):
    value = value + swap_row(value, 1)
    return value + swap_row(value, 2)


def scatter_row(partial, axis):
    me = lax.axis_index("row")
    half, core = me // 2, me % 2
    span = partial.shape[axis] // 4

    def piece(index):
        return lax.dynamic_slice_in_dim(partial, index * span, span, axis)

    far = swap_row(piece((1 - half) * 2 + 1 - core), 1)
    near = swap_row(piece(half * 2 + 1 - core), 1)
    away = piece((1 - half) * 2 + core).astype(jnp.float32) + far.astype(jnp.float32)
    came = swap_row(away.astype(BF), 2)
    kept = piece(half * 2 + core).astype(jnp.float32) + near.astype(jnp.float32)
    return kept + came.astype(jnp.float32)


def shift_col(value, distance):
    size = lax.axis_size("col")
    return lax.ppermute(value, "col", [(c, (c + distance) % size) for c in range(size)])


def gather_col(value):
    size = lax.axis_size("col")
    return jnp.stack([value] + [shift_col(value, k) for k in range(1, size)])


def in_order(blocks):
    size, me = blocks.shape[0], lax.axis_index("col")
    return jnp.stack(
        [lax.dynamic_index_in_dim(blocks, (me - k) % size, 0, False) for k in range(size)]
    )


def gather_row(value, other, axis):
    me = lax.axis_index("row")
    half, core = me // 2, me % 2
    beside = swap_row(value, 1)
    across = swap_row(other, 1)

    def pick(x, c):
        same = jnp.where(core == c, value, beside)
        away = jnp.where(core == c, other, across)
        return jnp.where(half == x, same, away)

    return jnp.concatenate([pick(0, 0), pick(0, 1), pick(1, 0), pick(1, 1)], axis=axis)


def apply_norm(values, totals, shift, scale):
    totals = totals.reshape(2, *values.shape[:3])
    mean = totals[0] / D
    variance = totals[1] / D - mean * mean
    normed = (values - mean[..., None]) * lax.rsqrt(variance + eps)[..., None]
    return (normed * (1.0 + scale[None, :, None]) + shift[None, :, None]).astype(BF)


def moments(values):
    return jnp.stack([jnp.sum(values, axis=-1), jnp.sum(values * values, axis=-1)]).reshape(2, -1)


def attend(q, k, v):
    scores = jnp.einsum("bhqd,bhkd->bhqk", q, k, preferred_element_type=jnp.float32)
    scores = scores / jnp.sqrt(jnp.float32(HEAD_DIM))
    weights = jnp.exp(scores - jnp.max(scores, axis=-1, keepdims=True))
    denom = jnp.sum(weights, axis=-1)
    mixed = jnp.einsum(
        "bhqk,bhkd->bhqd", weights.astype(BF), v, preferred_element_type=jnp.float32
    )
    return (mixed / denom[..., None]).astype(BF)


GROUPS = 2


def head_layer(clip_tokens, modulation, w_qkv, w_out, w_up, up_bias, w_down, guide_num):
    branches = modulation.shape[0]
    feat_rows, _, head_cols = w_qkv.shape
    mine = head_cols // 4
    heads = mine // HEAD_DIM
    here = clip_tokens.shape[0] // branches
    wide = branches // GROUPS
    cols = lax.axis_size("col")
    w_flat = w_qkv.reshape(feat_rows, 3, 4, mine).transpose(0, 2, 1, 3).reshape(feat_rows, -1)
    by_branch = clip_tokens.reshape(here, branches, feat_rows).transpose(1, 0, 2)
    guide = guide_num.astype(jnp.float32) / 4.0
    gate = guide[:, None] * modulation[:, 5]
    parts = [slice(g * wide, (g + 1) * wide) for g in range(GROUPS)]
    tokens = cols * wide * here
    x_parts = [by_branch[p].reshape(wide * here, feat_rows) for p in parts]
    gathered = [lax.all_gather(x, "col", axis=0, tiled=True) for x in x_parts]
    gathered[0], w_flat = lax.optimization_barrier((gathered[0], w_flat))

    def project(g):
        mod = modulation[parts[g]]
        x_all = gathered[g].astype(jnp.float32).reshape(cols, wide, here, feat_rows)
        first = apply_norm(x_all, sum_over_row(moments(x_all)), mod[:, 0], mod[:, 1])
        first = first.reshape(tokens, feat_rows)
        partial = jnp.dot(first, w_flat, preferred_element_type=jnp.float32).astype(BF)
        return scatter_row(partial, 1).astype(BF)

    def attention(g, qkv):
        shaped = qkv.reshape(cols, wide, here, 3, heads, HEAD_DIM).transpose(3, 1, 4, 0, 2, 5)
        shaped = shaped.reshape(3, wide, heads, cols * here, HEAD_DIM)
        att = attend(shaped[0], shaped[1], shaped[2])
        att = att.reshape(wide, heads, cols, here, HEAD_DIM).transpose(2, 0, 3, 1, 4)
        att = att.reshape(tokens, mine)
        att_all = gather_row(att, swap_row(att, 2), 1)
        partial = jnp.dot(att_all, w_out, preferred_element_type=jnp.float32).astype(BF)
        return lax.psum_scatter(partial, "col", scatter_dimension=0, tiled=True)

    def residual(g, out):
        mod = modulation[parts[g]]
        x = x_parts[g].astype(jnp.float32).reshape(1, wide, here, feat_rows)
        out = out.astype(jnp.float32).reshape(1, wide, here, feat_rows)
        resid = x + mod[None, :, 2, None] * out
        second = apply_norm(resid, sum_over_row(moments(resid)), mod[:, 3], mod[:, 4])
        second = second.reshape(wide * here, feat_rows)
        mixed = jnp.sum(resid[0] * guide[parts[g]][:, None, None], axis=0)
        if g < GROUPS - 1:
            return mixed, gather_col(second).reshape(tokens, feat_rows)
        return mixed, lax.all_gather(second, "col", axis=0, tiled=True)

    def expand(g, second_all):
        partial = jnp.dot(second_all, w_up, preferred_element_type=jnp.float32).astype(BF)
        up = scatter_row(partial, 0)
        act = jax.nn.gelu(up + up_bias[None], approximate=True).astype(BF)
        return act, swap_row(act, 2)

    def contract(g, act):
        down = jnp.dot(gather_row(act[0], act[1], 0), w_down, preferred_element_type=jnp.float32)
        down = down.reshape(cols, wide, here, feat_rows)
        down = sum(down[:, b] * gate[parts[g]][b] for b in range(wide))
        return in_order(down) if g < GROUPS - 1 else down

    every = range(GROUPS)
    qkv, acts = [], []
    for g in every:
        if g:
            gathered[g], qkv[-1] = lax.optimization_barrier((gathered[g], qkv[-1]))
        qkv.append(project(g))
    outs = [attention(g, qkv[g]) for g in every]
    mixed, seconds = [], []
    for g in every:
        out = outs[g]
        if g:
            out, seconds[-1] = lax.optimization_barrier((out, seconds[-1]))
        kept, second = residual(g, out)
        mixed.append(kept)
        seconds.append(second)
    for g in every:
        second = seconds[g]
        if g:
            second, acts[-1] = lax.optimization_barrier((second, acts[-1]))
        acts.append(expand(g, second))
    total = sum(contract(g, acts[g]) for g in every)
    total = total.astype(BF).reshape(cols * here, feat_rows)
    mlp = lax.psum_scatter(total, "col", scatter_dimension=0, tiled=True)
    return (sum(mixed) + mlp.astype(jnp.float32)).astype(BF)


def on_device(*args):
    heads_here = args[2].shape[2] // HEAD_DIM
    if lax.axis_size("row") == 4 and heads_here % 4 == 0:
        return head_layer(*args)
    return general_layer(*args)


def solution(mesh):
    in_specs = (
        P(("clips", "col"), "row"),
        P("clips", None, "row"),
        P("row", None, "col"),
        P("col", "row"),
        P("row", "col"),
        P("col"),
        P("col", "row"),
        P("clips"),
    )
    out_specs = P(("clips", "col"), "row")
    return jax.shard_map(
        on_device, mesh=mesh, in_specs=in_specs, out_specs=out_specs, check_vma=False
    )
```

```python
import jax
import jax.numpy as jnp
from jax import lax
from jax.sharding import PartitionSpec as P

D = 6144
HEAD_DIM = 128


eps = 1e-06


def normalize(values, shift, scale):
    totals = lax.psum((jnp.sum(values, axis=1), jnp.sum(values * values, axis=1)), "row")
    mean = totals[0] / D
    variance = totals[1] / D - mean * mean
    normed = (values - mean[:, None]) * lax.rsqrt(variance + eps)[:, None]
    branches = shift.shape[0]
    shaped = normed.reshape(-1, branches, values.shape[1]) * (1.0 + scale[None]) + shift[None]
    return shaped.reshape(values.shape)


def general_layer(clip_tokens, modulation, w_qkv, w_out, w_up, up_bias, w_down, guide_num):
    branches = modulation.shape[0]
    feat_rows = w_qkv.shape[0]
    head_cols = w_qkv.shape[2]
    heads_here = head_cols // HEAD_DIM
    x_rows = clip_tokens.astype(jnp.float32)
    first = normalize(x_rows, modulation[:, 0], modulation[:, 1]).astype(jnp.bfloat16)
    w_flat = w_qkv.reshape(feat_rows, 3 * head_cols)
    partial_qkv = jnp.dot(
        lax.all_gather(first, "col", axis=0, tiled=True), w_flat, preferred_element_type=jnp.float32
    )
    scale_score = 1.0 / jnp.sqrt(jnp.float32(HEAD_DIM))
    qkv = lax.psum_scatter(partial_qkv.astype(jnp.bfloat16), "row", scatter_dimension=0, tiled=True)
    query3 = qkv[:, :head_cols].reshape(-1, heads_here, HEAD_DIM)
    query_rows = query3.shape[0]
    piece = (
        lax.all_gather(qkv[:, head_cols : 2 * head_cols], "row", axis=0, tiled=True),
        lax.all_gather(qkv[:, 2 * head_cols :], "row", axis=0, tiled=True),
    )
    top = jnp.full((heads_here, query_rows), -1e30, jnp.float32)
    rows = piece[0].shape[0]
    key_heads = piece[0].reshape(rows, heads_here, HEAD_DIM)
    value_heads = piece[1].reshape(rows, heads_here, HEAD_DIM)
    scores = (
        jnp.einsum("qhd,khd->hqk", query3, key_heads, preferred_element_type=jnp.float32)
        * scale_score
    )
    query_branch = jnp.arange(query3.shape[0], dtype=jnp.int32) % branches
    key_branch = jnp.arange(rows, dtype=jnp.int32) % branches
    allowed = (query_branch[:, None] == key_branch[None, :])[None]
    masked = jnp.where(allowed, scores, -1e30)
    new_top = jnp.maximum(top, jnp.max(masked, axis=-1))
    weights = jnp.where(allowed, jnp.exp(masked - new_top[..., None]), 0.0)
    denom = jnp.sum(weights, axis=-1)
    accum = jnp.einsum(
        "hqk,khd->hqd",
        weights.astype(jnp.bfloat16),
        value_heads,
        preferred_element_type=jnp.float32,
    )
    att = (accum / denom[..., None]).transpose(1, 0, 2).reshape(-1, head_cols).astype(jnp.bfloat16)
    partial_out = jnp.dot(
        lax.all_gather(att, "row", axis=0, tiled=True), w_out, preferred_element_type=jnp.float32
    )
    out_rows = lax.psum_scatter(
        partial_out.astype(jnp.bfloat16), "col", scatter_dimension=0, tiled=True
    ).astype(jnp.float32)
    by_branch = x_rows.shape[0] // branches
    resid = (
        x_rows.reshape(by_branch, branches, feat_rows)
        + modulation[None, :, 2] * out_rows.reshape(by_branch, branches, feat_rows)
    ).reshape(x_rows.shape)
    second = normalize(resid, modulation[:, 3], modulation[:, 4]).astype(jnp.bfloat16)
    partial_up = jnp.dot(
        lax.all_gather(second, "col", axis=0, tiled=True), w_up, preferred_element_type=jnp.float32
    )
    up_rows = lax.psum_scatter(
        partial_up.astype(jnp.bfloat16), "row", scatter_dimension=0, tiled=True
    ).astype(jnp.float32)
    act = jax.nn.gelu(up_rows + up_bias[None], approximate=True).astype(jnp.bfloat16)
    partial_down = jnp.dot(
        lax.all_gather(act, "row", axis=0, tiled=True), w_down, preferred_element_type=jnp.float32
    )
    guide_weights = guide_num.astype(jnp.float32) / 4.0
    weights_gate = guide_weights[:, None] * modulation[:, 5]
    combined = jnp.sum(partial_down.reshape(-1, branches, feat_rows) * weights_gate[None], axis=1)
    mlp_rows = lax.psum_scatter(
        combined.astype(jnp.bfloat16), "col", scatter_dimension=0, tiled=True
    ).astype(jnp.float32)
    resid_mix = jnp.sum(
        resid.reshape(by_branch, branches, feat_rows) * guide_weights[None, :, None], axis=1
    )
    return (resid_mix + mlp_rows).astype(jnp.bfloat16)


BF = jnp.bfloat16


def swap_row(value, distance):
    size = lax.axis_size("row")
    return lax.ppermute(value, "row", [(r, r ^ distance) for r in range(size)])


def sum_over_row(value):
    value = value + swap_row(value, 1)
    return value + swap_row(value, 2)


def scatter_row(partial, axis):
    me = lax.axis_index("row")
    half, core = me // 2, me % 2
    span = partial.shape[axis] // 4

    def piece(index):
        return lax.dynamic_slice_in_dim(partial, index * span, span, axis)

    far = swap_row(piece((1 - half) * 2 + 1 - core), 1)
    near = swap_row(piece(half * 2 + 1 - core), 1)
    away = piece((1 - half) * 2 + core).astype(jnp.float32) + far.astype(jnp.float32)
    came = swap_row(away.astype(BF), 2)
    kept = piece(half * 2 + core).astype(jnp.float32) + near.astype(jnp.float32)
    return kept + came.astype(jnp.float32)


def shift_col(value, distance):
    size = lax.axis_size("col")
    return lax.ppermute(value, "col", [(c, (c + distance) % size) for c in range(size)])


def gather_col(value):
    size = lax.axis_size("col")
    return jnp.stack([value] + [shift_col(value, k) for k in range(1, size)])


def in_order(blocks):
    size, me = blocks.shape[0], lax.axis_index("col")
    return jnp.stack(
        [lax.dynamic_index_in_dim(blocks, (me - k) % size, 0, False) for k in range(size)]
    )


def gather_row(value, other, axis):
    me = lax.axis_index("row")
    half, core = me // 2, me % 2
    beside = swap_row(value, 1)
    across = swap_row(other, 1)

    def pick(x, c):
        same = jnp.where(core == c, value, beside)
        away = jnp.where(core == c, other, across)
        return jnp.where(half == x, same, away)

    return jnp.concatenate([pick(0, 0), pick(0, 1), pick(1, 0), pick(1, 1)], axis=axis)


def apply_norm(values, totals, shift, scale):
    totals = totals.reshape(2, *values.shape[:3])
    mean = totals[0] / D
    variance = totals[1] / D - mean * mean
    normed = (values - mean[..., None]) * lax.rsqrt(variance + eps)[..., None]
    return (normed * (1.0 + scale[None, :, None]) + shift[None, :, None]).astype(BF)


def moments(values):
    return jnp.stack([jnp.sum(values, axis=-1), jnp.sum(values * values, axis=-1)]).reshape(2, -1)


def attend(q, k, v):
    scores = jnp.einsum("bhqd,bhkd->bhqk", q, k, preferred_element_type=jnp.float32)
    scores = scores / jnp.sqrt(jnp.float32(HEAD_DIM))
    weights = jnp.exp(scores - jnp.max(scores, axis=-1, keepdims=True))
    denom = jnp.sum(weights, axis=-1)
    mixed = jnp.einsum(
        "bhqk,bhkd->bhqd", weights.astype(BF), v, preferred_element_type=jnp.float32
    )
    return (mixed / denom[..., None]).astype(BF)


GROUPS = 2


def head_layer(clip_tokens, modulation, w_qkv, w_out, w_up, up_bias, w_down, guide_num):
    branches = modulation.shape[0]
    feat_rows, _, head_cols = w_qkv.shape
    mine = head_cols // 4
    heads = mine // HEAD_DIM
    here = clip_tokens.shape[0] // branches
    wide = branches // GROUPS
    cols = lax.axis_size("col")
    w_flat = w_qkv.reshape(feat_rows, 3, 4, mine).transpose(0, 2, 1, 3).reshape(feat_rows, -1)
    by_branch = clip_tokens.reshape(here, branches, feat_rows).transpose(1, 0, 2)
    guide = guide_num.astype(jnp.float32) / 4.0
    gate = guide[:, None] * modulation[:, 5]
    parts = [slice(g * wide, (g + 1) * wide) for g in range(GROUPS)]
    tokens = cols * wide * here
    x_parts = [by_branch[p].reshape(wide * here, feat_rows) for p in parts]
    gathered = [lax.all_gather(x, "col", axis=0, tiled=True) for x in x_parts]
    gathered[0], w_flat = lax.optimization_barrier((gathered[0], w_flat))

    def project(g):
        mod = modulation[parts[g]]
        x_all = gathered[g].astype(jnp.float32).reshape(cols, wide, here, feat_rows)
        first = apply_norm(x_all, sum_over_row(moments(x_all)), mod[:, 0], mod[:, 1])
        first = first.reshape(tokens, feat_rows)
        partial = jnp.dot(first, w_flat, preferred_element_type=jnp.float32).astype(BF)
        return scatter_row(partial, 1).astype(BF)

    def attention(g, qkv):
        shaped = qkv.reshape(cols, wide, here, 3, heads, HEAD_DIM).transpose(3, 1, 4, 0, 2, 5)
        shaped = shaped.reshape(3, wide, heads, cols * here, HEAD_DIM)
        att = attend(shaped[0], shaped[1], shaped[2])
        att = att.reshape(wide, heads, cols, here, HEAD_DIM).transpose(2, 0, 3, 1, 4)
        att = att.reshape(tokens, mine)
        att_all = gather_row(att, swap_row(att, 2), 1)
        partial = jnp.dot(att_all, w_out, preferred_element_type=jnp.float32).astype(BF)
        return lax.psum_scatter(partial, "col", scatter_dimension=0, tiled=True)

    def residual(g, out):
        mod = modulation[parts[g]]
        x = x_parts[g].astype(jnp.float32).reshape(1, wide, here, feat_rows)
        out = out.astype(jnp.float32).reshape(1, wide, here, feat_rows)
        resid = x + mod[None, :, 2, None] * out
        second = apply_norm(resid, sum_over_row(moments(resid)), mod[:, 3], mod[:, 4])
        second = second.reshape(wide * here, feat_rows)
        mixed = jnp.sum(resid[0] * guide[parts[g]][:, None, None], axis=0)
        if g:
            seconds[-1], second = lax.optimization_barrier((seconds[-1], second))
        if g < GROUPS - 1:
            return mixed, gather_col(second).reshape(tokens, feat_rows)
        return mixed, lax.all_gather(second, "col", axis=0, tiled=True)

    def expand(g, second_all):
        partial = jnp.dot(second_all, w_up, preferred_element_type=jnp.float32).astype(BF)
        if g:
            before = acts[g - 1]
            partial, other = lax.optimization_barrier((partial, before[1]))
            acts[g - 1] = (before[0], other)
        up = scatter_row(partial, 0)
        act = jax.nn.gelu(up + up_bias[None], approximate=True).astype(BF)
        return act, swap_row(act, 2)

    def contract(g, act):
        down = jnp.dot(gather_row(act[0], act[1], 0), w_down, preferred_element_type=jnp.float32)
        down = down.reshape(cols, wide, here, feat_rows)
        down = sum(down[:, b] * gate[parts[g]][b] for b in range(wide))
        return in_order(down) if g < GROUPS - 1 else down

    every = range(GROUPS)
    qkv, acts = [], []
    for g in every:
        if g:
            gathered[g], qkv[-1] = lax.optimization_barrier((gathered[g], qkv[-1]))
        qkv.append(project(g))
    outs = [attention(g, qkv[g]) for g in every]
    mixed, seconds = [], []
    for g in every:
        out = outs[g]
        if g:
            out, seconds[-1] = lax.optimization_barrier((out, seconds[-1]))
        kept, second = residual(g, out)
        mixed.append(kept)
        seconds.append(second)
    for g in every:
        second = seconds[g]
        if g:
            second, act = lax.optimization_barrier((second, acts[-1][0]))
            acts[-1] = (act, acts[-1][1])
        acts.append(expand(g, second))
    total = sum(contract(g, acts[g]) for g in every)
    total = total.astype(BF).reshape(cols * here, feat_rows)
    mlp = lax.psum_scatter(total, "col", scatter_dimension=0, tiled=True)
    return (sum(mixed) + mlp.astype(jnp.float32)).astype(BF)


def on_device(*args):
    heads_here = args[2].shape[2] // HEAD_DIM
    if lax.axis_size("row") == 4 and heads_here % 4 == 0:
        return head_layer(*args)
    return general_layer(*args)


def solution(mesh):
    in_specs = (
        P(("clips", "col"), "row"),
        P("clips", None, "row"),
        P("row", None, "col"),
        P("col", "row"),
        P("row", "col"),
        P("col"),
        P("col", "row"),
        P("clips"),
    )
    out_specs = P(("clips", "col"), "row")
    return jax.shard_map(
        on_device, mesh=mesh, in_specs=in_specs, out_specs=out_specs, check_vma=False
    )
```
